1024 devices in a mesh: seq: 64 (over x, z), tp: 16 (over y, core).
Axes of the slice: x: 4, y: 8, z: 16, core: 2. Of those that a mesh axis runs over, the one named last changes fastest.
Arguments:
- queries: bfloat16 [16384, 8192], P('seq', 'tp'), may hold values from -6 to 6
- keys: bfloat16 [16384, 8192], P('seq', 'tp'), may hold values from -6 to 6
- values: bfloat16 [16384, 8192], P('seq', 'tp'), may hold values from -6 to 6
- norm_gain: float32 [128], replicated, may hold values from 0.1 to 1.9
- out_weight: bfloat16 [8192, 8192], P(None, 'tp'), may hold values from -0.0625 to 0.0625
Outputs:
- layer_out: bfloat16 [16384, 8192], P('seq', 'tp')
The draws below stay inside these ranges and needn't reach their ends.
All inputs are finite; a program needn't handle non-finite values.
Results may differ from the reference program's by a relative error of at most 0.0058.
Values may be sent and summed in bfloat16 or wider, within the bound.
No kernel may reach another device: no remote copies, remote signals or barrier semaphores. Data moves between devices by JAX's collectives and lax.ppermute only.
A program may use at most 32 MiB of HBM per device.

```python
import jax
import jax.numpy as jnp
from jax import lax

D = 8192
HEADS = 64
DH = 128
TOK_DEV = 256
TOKENS = 16384
N_SEQ = 64


def block_levels(rng, shape, cuts, smallest, top_value):
    def one(axis_at, shards_of):
        draws = jax.random.uniform(jax.random.fold_in(jax.random.fold_in(rng, 6), axis_at), (shards_of,), jnp.float32, smallest / len(cuts), top_value / len(cuts))
        return jnp.repeat(jnp.exp(draws), shape[axis_at] // shards_of).reshape((-1,) + (1,) * (len(shape) - axis_at - 1))

    gain = one(*cuts[0])
    for cut in cuts[1:]:
        gain = gain * one(*cut)
    return gain


def gaussian(key, extent, scale, most, shards=(), held_as=jnp.bfloat16):
    values = scale * jax.random.normal(key, extent, jnp.float32)
    if shards:
        values = values * block_levels(key, extent, shards, -0.22, 0.18)
    return jnp.clip(values, -most, most).astype(held_as)


def setup_inputs(seed: int = 0) -> dict:
    key_of = jax.random.split(jax.random.key(seed), 6)
    queries = gaussian(key_of[0], (TOKENS, D), 1.0, 6.0, ((0, 64), (1, 16)))
    keys = gaussian(key_of[1], (TOKENS, D), 1.0, 6.0, ((0, 64), (1, 16)))
    values = gaussian(key_of[2], (TOKENS, D), 1.0, 6.0, ((0, 64), (1, 16)))
    norm_gain = jnp.clip(1.0 + 0.18 * jax.random.normal(key_of[3], (DH,), jnp.float32), 0.1, 1.9)
    out_weight = gaussian(key_of[4], (D, D), D ** -0.5, 0.0625, ((1, 16),))
    return dict(queries=queries, keys=keys, values=values, norm_gain=norm_gain, out_weight=out_weight)


epsilon = 1e-06

def head_output(bundle, norm_gain):
    q_head, k_head, v_head = bundle
    q_float = q_head.astype(jnp.float32)
    k_float = k_head.astype(jnp.float32)
    v_float = v_head.astype(jnp.float32)
    states = jnp.einsum('ctk,ctv->ckv', k_float, v_float)
    running = jnp.cumsum(states, axis=0)
    prefix = jnp.concatenate([jnp.zeros_like(states[:1]), running[:-1]], axis=0)
    prefix_batch = lax.optimization_barrier(prefix.astype(jnp.bfloat16)).astype(jnp.float32)
    carried_state = jnp.einsum('ctk,ckv->ctv', q_float, prefix_batch)
    scores = jnp.einsum('ctk,csk->cts', q_float, k_float)
    row_ids = lax.broadcasted_iota(jnp.int32, (TOK_DEV, TOK_DEV), 0)
    col_ids = lax.broadcasted_iota(jnp.int32, (TOK_DEV, TOK_DEV), 1)
    causal = col_ids <= row_ids
    scores = jnp.where(causal[None], scores, jnp.float32(0.0))
    scores_b = lax.optimization_barrier(scores.astype(jnp.bfloat16)).astype(jnp.float32)
    within = jnp.einsum('cts,csv->ctv', scores_b, v_float)
    attended = carried_state + within
    inverse = lax.rsqrt(lax.optimization_barrier(jnp.mean(attended * attended, axis=-1, keepdims=True)) + epsilon)
    return (attended * inverse * norm_gain).astype(jnp.bfloat16)

def split_heads(array):
    return array.reshape(N_SEQ, TOK_DEV, HEADS, DH).transpose(2, 0, 1, 3)

def reference(queries, keys, values, norm_gain, out_weight):

    def one_head(bundle):
        return head_output(bundle, norm_gain)
    normed = lax.map(one_head, (split_heads(queries), split_heads(keys), split_heads(values)))
    normed = normed.transpose(1, 2, 0, 3).reshape(TOKENS, D)
    return jnp.dot(normed, out_weight, preferred_element_type=jnp.float32).astype(jnp.bfloat16)
```

```python
import functools

import jax
import jax.numpy as jnp
from jax import lax
from jax.experimental import pallas as pl
from jax.experimental.pallas import tpu as pltpu
from jax.sharding import PartitionSpec as P

DH = 128

epsilon = 1e-06


VMEM = pl.BlockSpec(memory_space=pltpu.VMEM)
SMEM = pl.BlockSpec(memory_space=pltpu.SMEM)
PARAMS = pltpu.CompilerParams(vmem_limit_bytes=12 * 2**20)
WIDE = pltpu.CompilerParams(vmem_limit_bytes=50 * 2**20)
HBM = pl.BlockSpec(memory_space=pltpu.HBM)


def state_kernel(k_ref, v_ref, s_ref):
    heads = k_ref.shape[1] // DH
    for h in range(heads):
        cols = slice(h * DH, (h + 1) * DH)
        s_ref[cols, :] = lax.dot_general(
            k_ref[:, cols],
            v_ref[:, cols],
            (((0,), (0,)), ((), ())),
            preferred_element_type=jnp.float32,
        ).astype(s_ref.dtype)


def scan_kernel(a_ref, p_ref):
    total = jnp.zeros(a_ref.shape[1:], jnp.float32)
    for c in range(a_ref.shape[0]):
        p_ref[c] = total.astype(p_ref.dtype)
        total = total + a_ref[c].astype(jnp.float32)


def attend_kernel(q_ref, k_ref, v_ref, p_ref, g_ref, o_ref):
    rows = q_ref.shape[0]
    row_ids = lax.broadcasted_iota(jnp.int32, (rows, rows), 0)
    col_ids = lax.broadcasted_iota(jnp.int32, (rows, rows), 1)
    causal = col_ids <= row_ids
    for h in range(q_ref.shape[1] // DH):
        cols = slice(h * DH, (h + 1) * DH)
        q, k, v = q_ref[:, cols], k_ref[:, cols], v_ref[:, cols]
        scores = lax.dot_general(
            q, k, (((1,), (1,)), ((), ())), preferred_element_type=jnp.float32
        )
        scores = jnp.where(causal, scores, 0.0).astype(jnp.bfloat16)
        attended = jnp.dot(q, p_ref[cols, :], preferred_element_type=jnp.float32)
        attended = attended + jnp.dot(scores, v, preferred_element_type=jnp.float32)
        mean = jnp.mean(attended * attended, axis=-1, keepdims=True)
        o_ref[:, cols] = (attended * lax.rsqrt(mean + epsilon) * g_ref[...]).astype(o_ref.dtype)


def source(me, ring, step, other):
    core = lax.rem(me, 2)
    at = lax.div(me, 2) + jnp.where(core == 0, ring - step, step)
    return 2 * lax.rem(at, ring) + (1 - core if other else core)


def project_kernel(ring, sources, terms, seeded, *refs):
    blocks = len(sources)
    accs = 1 + max(t[2] for t in terms)
    me = refs[0][0]
    block_refs = refs[1 : 1 + blocks]
    weight_refs = refs[1 + blocks : 3 + blocks]
    pos = 3 + blocks
    seeds = refs[pos : pos + accs] if seeded else None
    pos += accs if seeded else 0
    outs = refs[pos : pos + accs]
    slots, sems = refs[pos + accs :]
    depth = slots.shape[1]
    copies = []
    for n, (b, w, _) in enumerate(terms):
        at = pl.multiple_of(source(me, ring, *sources[b]) * depth, depth)
        copy = pltpu.make_async_copy(
            weight_refs[w].at[pl.ds(at, depth), :], slots.at[n], sems.at[n]
        )
        copy.start()
        copies.append(copy)
    started = [seeded] * accs
    for n, (b, _, a) in enumerate(terms):
        copies[n].wait()
        part = jnp.dot(block_refs[b][...], slots[n], preferred_element_type=jnp.float32)
        if started[a]:
            part = (outs[a][...] if started[a] == 2 else seeds[a][...]) + part
        outs[a][...] = part
        started[a] = 2


def project(me, ring, blocks, sources, weights, terms, seeds=None):
    rows, depth = blocks[0].shape
    cols = weights[0].shape[1]
    accs = 1 + max(t[2] for t in terms)
    seeds = list(seeds or [])
    flops = 2 * rows * depth * cols * len(terms)
    return pl.pallas_call(
        functools.partial(project_kernel, ring, sources, terms, bool(seeds)),
        out_shape=[jax.ShapeDtypeStruct((rows, cols), jnp.float32)] * accs,
        in_specs=[SMEM] + [VMEM] * len(blocks) + [HBM, HBM] + [VMEM] * len(seeds),
        out_specs=[VMEM] * accs,
        scratch_shapes=[
            pltpu.VMEM((len(terms), depth, cols), weights[0].dtype),
            pltpu.SemaphoreType.DMA((len(terms),)),
        ],
        compiler_params=WIDE,
        cost_estimate=pl.CostEstimate(
            flops=flops,
            bytes_accessed=len(terms) * depth * cols * 2,
            transcendentals=0,
        ),
    )(me.reshape(1), *blocks, *weights, *seeds)


def call(kernel, shape, dtype, args, flops):
    size = sum(a.size * a.dtype.itemsize for a in args)
    return pl.pallas_call(
        kernel,
        out_shape=jax.ShapeDtypeStruct(shape, dtype),
        in_specs=[VMEM] * len(args),
        out_specs=VMEM,
        compiler_params=PARAMS,
        cost_estimate=pl.CostEstimate(flops=flops, bytes_accessed=size, transcendentals=0),
    )(*args)


def on_device(queries, keys, values, norm_gain, out_weight):
    rows, width = queries.shape
    groups = lax.axis_size("seq")
    tp = lax.axis_size("tp")
    ring = tp // 2
    me = lax.axis_index("tp")
    partner = [(j, j ^ 1) for j in range(tp)]
    onward = [
        (2 * y + c, 2 * ((y + (1, -1)[c]) % ring) + c) for y in range(ring) for c in range(2)
    ]

    states = call(
        state_kernel, (width, DH), jnp.bfloat16, (keys, values), 2 * rows * width * DH
    )
    slices = states.reshape(groups, width // groups, DH)
    slices = lax.all_to_all(slices, "seq", 0, 0, tiled=True)
    prefix = call(scan_kernel, slices.shape, jnp.bfloat16, (slices,), slices.size)
    prefix = lax.all_to_all(prefix, "seq", 0, 0, tiled=True).reshape(width, DH)
    own = call(
        attend_kernel,
        (rows, width),
        jnp.bfloat16,
        (queries, keys, values, prefix, norm_gain.reshape(1, DH)),
        8 * rows * rows * width,
    )
    their_weight = lax.ppermute(out_weight, "tp", partner)
    weights = (out_weight, their_weight)

    half = (ring - 1) // 2
    tie = lax.optimization_barrier
    both = [(0, 0, 0), (1, 0, 0), (0, 1, 1), (1, 1, 1)]
    first = [own, lax.ppermute(own, "tp", onward)]
    second = [lax.ppermute(own, "tp", partner)]
    (mine,) = project(
        me,
        ring,
        (own, second[0]),
        [(0, False), (0, True)],
        weights,
        [(0, 0, 0), (1, 0, 0)],
    )
    accs = (mine, jnp.zeros((rows, width), jnp.float32))
    for s in range(1, half + 1):
        second.append(lax.ppermute(second[-1], "tp", onward))
        first[-1], accs = tie((first[-1], accs))
        first.append(lax.ppermute(first[-1], "tp", onward))
        accs = project(
            me,
            ring,
            (first[s], second[s]),
            [(s, False), (s, True)],
            weights,
            both,
            accs,
        )
    last = half + 1
    (theirs,) = project(
        me,
        ring,
        (first[last],), [(last, False)], weights, [(0, 1, 0)], accs[1:]
    )
    returned = lax.ppermute(theirs, "tp", partner)
    (mine,) = project(me, ring, (first[last],), [(last, False)], weights, [(0, 0, 0)], accs[:1])
    return (mine + returned).astype(jnp.bfloat16)


def solution(mesh):
    return jax.shard_map(
        on_device,
        mesh=mesh,
        in_specs=(P("seq", "tp"), P("seq", "tp"), P("seq", "tp"), P(), P(None, "tp")),
        out_specs=P("seq", "tp"),
        check_vma=False,
    )
```

```python
import functools

import jax
import jax.numpy as jnp
from jax import lax
from jax.experimental import pallas as pl
from jax.experimental.pallas import tpu as pltpu
from jax.sharding import PartitionSpec as P

DH = 128

epsilon = 1e-06


VMEM = pl.BlockSpec(memory_space=pltpu.VMEM)
SMEM = pl.BlockSpec(memory_space=pltpu.SMEM)
PARAMS = pltpu.CompilerParams(vmem_limit_bytes=12 * 2**20)
WIDE = pltpu.CompilerParams(vmem_limit_bytes=50 * 2**20)
HBM = pl.BlockSpec(memory_space=pltpu.HBM)


def local_kernel(q_ref, k_ref, v_ref, g_ref, s_ref, w_ref, qo_ref, go_ref):
    rows = q_ref.shape[0]
    heads = [slice(h, h + DH) for h in range(0, q_ref.shape[1], DH)]
    for cols in heads:
        s_ref[cols, :] = lax.dot_general(
            k_ref[:, cols],
            v_ref[:, cols],
            (((0,), (0,)), ((), ())),
            preferred_element_type=jnp.float32,
        ).astype(s_ref.dtype)
    row_ids = lax.broadcasted_iota(jnp.int32, (rows, rows), 0)
    col_ids = lax.broadcasted_iota(jnp.int32, (rows, rows), 1)
    causal = col_ids <= row_ids
    for cols in heads:
        scores = lax.dot_general(
            q_ref[:, cols],
            k_ref[:, cols],
            (((1,), (1,)), ((), ())),
            preferred_element_type=jnp.float32,
        )
        scores = jnp.where(causal, scores, 0.0).astype(jnp.bfloat16)
        w_ref[:, cols] = jnp.dot(scores, v_ref[:, cols], preferred_element_type=jnp.float32)
    qo_ref[...] = q_ref[...]
    go_ref[...] = g_ref[...]


def scan_kernel(a_ref, p_ref):
    total = jnp.zeros(a_ref.shape[1:], jnp.float32)
    for c in range(a_ref.shape[0]):
        p_ref[c] = total.astype(p_ref.dtype)
        total = total + a_ref[c].astype(jnp.float32)


def attend_kernel(q_ref, w_ref, p_ref, g_ref, o_ref):
    for h in range(0, q_ref.shape[1], DH):
        cols = slice(h, h + DH)
        attended = jnp.dot(q_ref[:, cols], p_ref[cols, :], preferred_element_type=jnp.float32)
        attended = attended + w_ref[:, cols]
        mean = jnp.mean(attended * attended, axis=-1, keepdims=True)
        o_ref[:, cols] = (attended * lax.rsqrt(mean + epsilon) * g_ref[...]).astype(o_ref.dtype)


def source(me, ring, step, other):
    core = lax.rem(me, 2)
    at = lax.div(me, 2) + jnp.where(core == 0, ring - step, step)
    return 2 * lax.rem(at, ring) + (1 - core if other else core)


def project_kernel(ring, sources, terms, seeded, *refs):
    blocks = len(sources)
    accs = 1 + max(t[2] for t in terms)
    me = refs[0][0]
    block_refs = refs[1 : 1 + blocks]
    weight_refs = refs[1 + blocks : 3 + blocks]
    pos = 3 + blocks
    seeds = refs[pos : pos + accs] if seeded else None
    pos += accs if seeded else 0
    outs = refs[pos : pos + accs]
    slots, sems = refs[pos + accs :]
    depth = slots.shape[1]
    copies = []
    for n, (b, w, _) in enumerate(terms):
        at = pl.multiple_of(source(me, ring, *sources[b]) * depth, depth)
        copy = pltpu.make_async_copy(
            weight_refs[w].at[pl.ds(at, depth), :], slots.at[n], sems.at[n]
        )
        copy.start()
        copies.append(copy)
    started = [seeded] * accs
    for n, (b, _, a) in enumerate(terms):
        copies[n].wait()
        part = jnp.dot(block_refs[b][...], slots[n], preferred_element_type=jnp.float32)
        if started[a]:
            part = (outs[a][...] if started[a] == 2 else seeds[a][...]) + part
        outs[a][...] = part
        started[a] = 2


def project(me, ring, blocks, sources, weights, terms, seeds=None):
    rows, depth = blocks[0].shape
    cols = weights[0].shape[1]
    accs = 1 + max(t[2] for t in terms)
    seeds = list(seeds or [])
    flops = 2 * rows * depth * cols * len(terms)
    return pl.pallas_call(
        functools.partial(project_kernel, ring, sources, terms, bool(seeds)),
        out_shape=[jax.ShapeDtypeStruct((rows, cols), jnp.float32)] * accs,
        in_specs=[SMEM] + [VMEM] * len(blocks) + [HBM, HBM] + [VMEM] * len(seeds),
        out_specs=[VMEM] * accs,
        scratch_shapes=[
            pltpu.VMEM((len(terms), depth, cols), weights[0].dtype),
            pltpu.SemaphoreType.DMA((len(terms),)),
        ],
        compiler_params=WIDE,
        cost_estimate=pl.CostEstimate(
            flops=flops,
            bytes_accessed=len(terms) * depth * cols * 2,
            transcendentals=0,
        ),
    )(me.reshape(1), *blocks, *weights, *seeds)


def call(kernel, shape, dtype, args, flops):
    size = sum(a.size * a.dtype.itemsize for a in args)
    return pl.pallas_call(
        kernel,
        out_shape=jax.ShapeDtypeStruct(shape, dtype),
        in_specs=[VMEM] * len(args),
        out_specs=VMEM,
        compiler_params=PARAMS,
        cost_estimate=pl.CostEstimate(flops=flops, bytes_accessed=size, transcendentals=0),
    )(*args)


def local(queries, keys, values, gain):
    rows, width = queries.shape
    return pl.pallas_call(
        local_kernel,
        out_shape=[
            jax.ShapeDtypeStruct((width, DH), jnp.bfloat16),
            jax.ShapeDtypeStruct((rows, width), jnp.float32),
            jax.ShapeDtypeStruct((rows, width), queries.dtype),
            jax.ShapeDtypeStruct(gain.shape, gain.dtype),
        ],
        in_specs=[VMEM] * 4,
        out_specs=[VMEM] * 4,
        compiler_params=PARAMS,
        cost_estimate=pl.CostEstimate(
            flops=2 * rows * width * (DH + 2 * rows),
            bytes_accessed=3 * rows * width * 2,
            transcendentals=0,
        ),
    )(queries, keys, values, gain)


def on_device(queries, keys, values, norm_gain, out_weight):
    rows, width = queries.shape
    groups = lax.axis_size("seq")
    tp = lax.axis_size("tp")
    ring = tp // 2
    me = lax.axis_index("tp")
    partner = [(j, j ^ 1) for j in range(tp)]
    onward = [
        (2 * y + c, 2 * ((y + (1, -1)[c]) % ring) + c) for y in range(ring) for c in range(2)
    ]
    tie = lax.optimization_barrier

    their_weight = lax.ppermute(out_weight, "tp", partner)
    weights = (out_weight, their_weight)
    states, within, near_queries, gain = local(
        queries, keys, values, norm_gain.reshape(1, DH)
    )
    slices = states.reshape(groups, width // groups, DH)
    slices = lax.all_to_all(slices, "seq", 0, 0, tiled=True)
    prefix = call(scan_kernel, slices.shape, jnp.bfloat16, (slices,), slices.size)
    prefix = lax.all_to_all(prefix, "seq", 0, 0, tiled=True).reshape(width, DH)
    own = call(
        attend_kernel,
        (rows, width),
        jnp.bfloat16,
        (near_queries, within, prefix, gain),
        2 * rows * width * DH,
    )

    def multiply(block, step, other, terms, seeds=None):
        return project(me, ring, (block,), [(step, other)], weights, terms, seeds)

    half = (ring - 1) // 2
    both = [(0, 0, 0), (0, 1, 1)]
    first = lax.ppermute(own, "tp", onward)
    second = lax.ppermute(own, "tp", partner)
    (mine,) = multiply(own, 0, False, [(0, 0, 0)])
    second, mine = tie((second, mine))
    (mine,) = multiply(second, 0, True, [(0, 0, 0)], (mine,))
    sums = (mine, jnp.zeros((rows, width), jnp.float32))
    second = lax.ppermute(second, "tp", onward)
    for step in range(1, half + 1):
        first, sums = tie((first, sums))
        sums = multiply(first, step, False, both, sums)
        first = lax.ppermute(first, "tp", onward)
        second, sums = tie((second, sums))
        sums = multiply(second, step, True, both, sums)
        if step < half:
            second = lax.ppermute(second, "tp", onward)
    (theirs,) = multiply(first, half + 1, False, [(0, 1, 0)], sums[1:])
    returned = lax.ppermute(theirs, "tp", partner)
    (mine,) = multiply(first, half + 1, False, [(0, 0, 0)], sums[:1])
    return (mine + returned).astype(jnp.bfloat16)


def solution(mesh):
    return jax.shard_map(
        on_device,
        mesh=mesh,
        in_specs=(P("seq", "tp"), P("seq", "tp"), P("seq", "tp"), P(), P(None, "tp")),
        out_specs=P("seq", "tp"),
        check_vma=False,
    )
```

```python
import functools

import jax
import jax.numpy as jnp
from jax import lax
from jax.experimental import pallas as pl
from jax.experimental.pallas import tpu as pltpu
from jax.sharding import PartitionSpec as P

DH = 128

epsilon = 1e-06


VMEM = pl.BlockSpec(memory_space=pltpu.VMEM)
SMEM = pl.BlockSpec(memory_space=pltpu.SMEM)
PARAMS = pltpu.CompilerParams(vmem_limit_bytes=12 * 2**20)
WIDE = pltpu.CompilerParams(vmem_limit_bytes=50 * 2**20)
HBM = pl.BlockSpec(memory_space=pltpu.HBM)


def local_kernel(q_ref, k_ref, v_ref, g_ref, s_ref, w_ref, qo_ref, go_ref):
    rows = q_ref.shape[0]
    heads = [slice(h, h + DH) for h in range(0, q_ref.shape[1], DH)]
    for cols in heads:
        s_ref[cols, :] = lax.dot_general(
            k_ref[:, cols],
            v_ref[:, cols],
            (((0,), (0,)), ((), ())),
            preferred_element_type=jnp.float32,
        ).astype(s_ref.dtype)
    row_ids = lax.broadcasted_iota(jnp.int32, (rows, rows), 0)
    col_ids = lax.broadcasted_iota(jnp.int32, (rows, rows), 1)
    causal = col_ids <= row_ids
    for cols in heads:
        scores = lax.dot_general(
            q_ref[:, cols],
            k_ref[:, cols],
            (((1,), (1,)), ((), ())),
            preferred_element_type=jnp.float32,
        )
        scores = jnp.where(causal, scores, 0.0).astype(jnp.bfloat16)
        w_ref[:, cols] = jnp.dot(scores, v_ref[:, cols], preferred_element_type=jnp.float32)
    qo_ref[...] = q_ref[...]
    go_ref[...] = g_ref[...]


def scan_kernel(a_ref, p_ref):
    total = jnp.zeros(a_ref.shape[1:], jnp.float32)
    for c in range(a_ref.shape[0]):
        p_ref[c] = total.astype(p_ref.dtype)
        total = total + a_ref[c].astype(jnp.float32)


def attend_kernel(q_ref, w_ref, p_ref, g_ref, o_ref):
    for h in range(0, q_ref.shape[1], DH):
        cols = slice(h, h + DH)
        attended = jnp.dot(q_ref[:, cols], p_ref[cols, :], preferred_element_type=jnp.float32)
        attended = attended + w_ref[:, cols]
        mean = jnp.mean(attended * attended, axis=-1, keepdims=True)
        o_ref[:, cols] = (attended * lax.rsqrt(mean + epsilon) * g_ref[...]).astype(o_ref.dtype)


def source(me, ring, step, other):
    core = lax.rem(me, 2)
    at = lax.div(me, 2) + jnp.where(core == 0, ring - step, step)
    return 2 * lax.rem(at, ring) + (1 - core if other else core)


def project_kernel(ring, step, other, weights, seeded, me_ref, block_ref, *refs):
    count = len(weights)
    weight_refs, refs = refs[:2], refs[2:]
    seeds = refs[:count] if seeded else None
    outs = refs[count if seeded else 0 :][:count]
    slots, sems = refs[-2:]
    depth = slots.shape[1]
    at = pl.multiple_of(source(me_ref[0], ring, step, other) * depth, depth)
    copies = []
    for n, w in enumerate(weights):
        rows = weight_refs[w].at[pl.ds(at, depth), :]
        copies.append(pltpu.make_async_copy(rows, slots.at[n], sems.at[n]))
        copies[-1].start()
    for n in range(count):
        copies[n].wait()
        part = jnp.dot(block_ref[...], slots[n], preferred_element_type=jnp.float32)
        outs[n][...] = seeds[n][...] + part if seeded else part


def project(me, ring, step, other, block, columns, weights, seeds=()):
    rows, depth = block.shape
    cols = columns[0].shape[1]
    count = len(weights)
    return pl.pallas_call(
        functools.partial(project_kernel, ring, step, other, weights, bool(seeds)),
        out_shape=[jax.ShapeDtypeStruct((rows, cols), jnp.float32)] * count,
        in_specs=[SMEM, VMEM, HBM, HBM] + [VMEM] * len(seeds),
        out_specs=[VMEM] * count,
        scratch_shapes=[
            pltpu.VMEM((count, depth, cols), columns[0].dtype),
            pltpu.SemaphoreType.DMA((count,)),
        ],
        compiler_params=WIDE,
        cost_estimate=pl.CostEstimate(
            flops=2 * rows * depth * cols * count,
            bytes_accessed=count * depth * cols * 2,
            transcendentals=0,
        ),
    )(me.reshape(1), block, *columns, *seeds)


def pair_kernel(ring, step, me_ref, pair_ref, w_ref, seed_ref, *refs):
    more, (out_ref, slots, sems) = refs[:-3], refs[-3:]
    rows = seed_ref.shape[0]
    depth = slots.shape[1]
    chip = source(me_ref[0], ring, step, False) // 2
    copies = []
    for n in range(2):
        at = pl.multiple_of((2 * chip + n) * depth, depth)
        copies.append(pltpu.make_async_copy(w_ref.at[pl.ds(at, depth), :], slots.at[n], sems.at[n]))
        copies[-1].start()
    total = seed_ref[...]
    for ref in more:
        total = total + ref[...]
    for n in range(2):
        copies[n].wait()
        block = pair_ref[n * rows : (n + 1) * rows, :]
        total = total + jnp.dot(block, slots[n], preferred_element_type=jnp.float32)
    out_ref[...] = total.astype(out_ref.dtype)


def project_pair(me, ring, step, pair, weight, dtype, *seeds):
    rows, cols = seeds[0].shape
    depth = pair.shape[1]
    return pl.pallas_call(
        functools.partial(pair_kernel, ring, step),
        out_shape=jax.ShapeDtypeStruct((rows, cols), dtype),
        in_specs=[SMEM, VMEM, HBM] + [VMEM] * len(seeds),
        out_specs=VMEM,
        scratch_shapes=[
            pltpu.VMEM((2, depth, cols), weight.dtype),
            pltpu.SemaphoreType.DMA((2,)),
        ],
        compiler_params=WIDE,
        cost_estimate=pl.CostEstimate(
            flops=4 * rows * depth * cols,
            bytes_accessed=2 * depth * cols * 2,
            transcendentals=0,
        ),
    )(me.reshape(1), pair, weight, *seeds)


def call(kernel, shape, dtype, args, flops):
    size = sum(a.size * a.dtype.itemsize for a in args)
    return pl.pallas_call(
        kernel,
        out_shape=jax.ShapeDtypeStruct(shape, dtype),
        in_specs=[VMEM] * len(args),
        out_specs=VMEM,
        compiler_params=PARAMS,
        cost_estimate=pl.CostEstimate(flops=flops, bytes_accessed=size, transcendentals=0),
    )(*args)


def local(queries, keys, values, gain):
    rows, width = queries.shape
    return pl.pallas_call(
        local_kernel,
        out_shape=[
            jax.ShapeDtypeStruct((width, DH), jnp.bfloat16),
            jax.ShapeDtypeStruct((rows, width), jnp.float32),
            jax.ShapeDtypeStruct((rows, width), queries.dtype),
            jax.ShapeDtypeStruct(gain.shape, gain.dtype),
        ],
        in_specs=[VMEM] * 4,
        out_specs=[VMEM] * 4,
        compiler_params=PARAMS,
        cost_estimate=pl.CostEstimate(
            flops=2 * rows * width * (DH + 2 * rows),
            bytes_accessed=3 * rows * width * 2,
            transcendentals=0,
        ),
    )(queries, keys, values, gain)


def on_device(queries, keys, values, norm_gain, out_weight):
    rows, width = queries.shape
    groups = lax.axis_size("seq")
    tp = lax.axis_size("tp")
    ring = tp // 2
    me = lax.axis_index("tp")
    partner = [(j, j ^ 1) for j in range(tp)]
    onward = [
        (2 * y + c, 2 * ((y + (1, -1)[c]) % ring) + c) for y in range(ring) for c in range(2)
    ]
    across = [(s ^ 1, d) for s, d in onward]
    tie = lax.optimization_barrier

    states, within, near_queries, gain = local(
        queries, keys, values, norm_gain.reshape(1, DH)
    )
    weight, states = tie((out_weight, states))
    columns = (out_weight, lax.ppermute(weight, "tp", partner))
    slices = states.reshape(groups, width // groups, DH)
    slices = lax.all_to_all(slices, "seq", 0, 0, tiled=True)
    prefix = call(scan_kernel, slices.shape, jnp.bfloat16, (slices,), slices.size)
    prefix = lax.all_to_all(prefix, "seq", 0, 0, tiled=True).reshape(width, DH)
    own = call(
        attend_kernel,
        (rows, width),
        jnp.bfloat16,
        (near_queries, within, prefix, gain),
        2 * rows * width * DH,
    )

    halves = [[2 * y, 2 * y + 1] for y in range(ring)]
    half = (ring - 1) // 2

    def send(block, pairs):
        return lax.ppermute(block, "tp", pairs)

    def multiply(step, other, block, sums):
        return project(me, ring, step, other, block, columns, (0, 1), sums)

    first = send(own, onward)
    second = send(own, across)
    sums = multiply(0, False, own, ())
    for step in range(1, half + 1):
        first, sums = tie((first, sums))
        sums = multiply(step, False, first, sums)
        first = send(first, onward)
        second, sums = tie((second, sums))
        sums = multiply(step, True, second, sums)
        if step < half:
            second = send(second, onward)
    mine, theirs = sums
    returned = send(theirs, partner)
    first, returned = tie((first, returned))
    pair = lax.all_gather(first, "tp", axis=0, tiled=True, axis_index_groups=halves)
    return project_pair(me, ring, half + 1, pair, out_weight, jnp.bfloat16, mine, returned)


def solution(mesh):
    return jax.shard_map(
        on_device,
        mesh=mesh,
        in_specs=(P("seq", "tp"), P("seq", "tp"), P("seq", "tp"), P(), P(None, "tp")),
        out_specs=P("seq", "tp"),
        check_vma=False,
    )
```

```python
import functools

import jax
import jax.numpy as jnp
from jax import lax
from jax.experimental import pallas as pl
from jax.experimental.pallas import tpu as pltpu
from jax.sharding import PartitionSpec as P

DH = 128

epsilon = 1e-06


VMEM = pl.BlockSpec(memory_space=pltpu.VMEM)
SMEM = pl.BlockSpec(memory_space=pltpu.SMEM)
PARAMS = pltpu.CompilerParams(vmem_limit_bytes=12 * 2**20)
HBM = pl.BlockSpec(memory_space=pltpu.HBM)


def local_kernel(q_hbm, k_hbm, v_hbm, g_hbm, s_ref, w_ref, q_ref, g_ref, k_ref, v_ref, sems):
    pairs = ((k_hbm, k_ref), (v_hbm, v_ref), (q_hbm, q_ref), (g_hbm, g_ref))
    copies = [pltpu.make_async_copy(a, b, sems.at[n]) for n, (a, b) in enumerate(pairs)]
    for copy in copies:
        copy.start()
    rows = q_ref.shape[0]
    heads = [slice(h, h + DH) for h in range(0, q_ref.shape[1], DH)]
    copies[0].wait()
    copies[1].wait()
    for cols in heads:
        s_ref[cols, :] = lax.dot_general(
            k_ref[:, cols],
            v_ref[:, cols],
            (((0,), (0,)), ((), ())),
            preferred_element_type=jnp.float32,
        ).astype(s_ref.dtype)
    row_ids = lax.broadcasted_iota(jnp.int32, (rows, rows), 0)
    col_ids = lax.broadcasted_iota(jnp.int32, (rows, rows), 1)
    causal = col_ids <= row_ids
    copies[2].wait()
    copies[3].wait()
    for cols in heads:
        scores = lax.dot_general(
            q_ref[:, cols],
            k_ref[:, cols],
            (((1,), (1,)), ((), ())),
            preferred_element_type=jnp.float32,
        )
        scores = jnp.where(causal, scores, 0.0).astype(jnp.bfloat16)
        w_ref[:, cols] = jnp.dot(scores, v_ref[:, cols], preferred_element_type=jnp.float32)


def scan_kernel(a_ref, p_ref):
    total = jnp.zeros(a_ref.shape[1:], jnp.float32)
    for c in range(a_ref.shape[0]):
        p_ref[c] = total.astype(p_ref.dtype)
        total = total + a_ref[c].astype(jnp.float32)


def attend_kernel(q_ref, w_ref, p_ref, g_ref, o_ref):
    for h in range(0, q_ref.shape[1], DH):
        cols = slice(h, h + DH)
        attended = jnp.dot(q_ref[:, cols], p_ref[cols, :], preferred_element_type=jnp.float32)
        attended = attended + w_ref[:, cols]
        mean = jnp.mean(attended * attended, axis=-1, keepdims=True)
        o_ref[:, cols] = (attended * lax.rsqrt(mean + epsilon) * g_ref[...]).astype(o_ref.dtype)


def source(me, ring, step, other):
    core = lax.rem(me, 2)
    at = lax.div(me, 2) + jnp.where(core == 0, ring - step, step)
    return 2 * lax.rem(at, ring) + (1 - core if other else core)


def in_hbm(*arrays):
    return [pltpu.with_memory_space_constraint(a, pltpu.HBM) for a in arrays]


def fetch(weight_refs, rows, out_ref, sems):
    depth = out_ref.shape[1]
    copies = []
    for n, (w, block) in enumerate(rows):
        at = pl.multiple_of(block * depth, depth)
        source_rows = weight_refs[w].at[pl.ds(at, depth), :]
        copies.append(pltpu.make_async_copy(source_rows, out_ref.at[n], sems.at[n]))
        copies[-1].start()
    return copies


def wanted(me, ring, step, other):
    block = source(me, ring, step, other)
    if step <= (ring - 1) // 2:
        return [(0, block), (1, block)]
    chip = lax.div(block, 2)
    return [(0, 2 * chip), (0, 2 * chip + 1)]


def project_kernel(ring, here, then, first, me_ref, block_ref, w0_ref, w1_ref, *refs):
    me = me_ref[0]
    weights = (w0_ref, w1_ref)
    if first:
        outs, (ahead_ref, now_ref, sems, now_sems) = refs[:2], refs[2:]
        now = fetch(weights, wanted(me, ring, *here), now_ref, now_sems)
    else:
        now_ref, seeds, outs, (ahead_ref, sems) = refs[0], refs[1:3], refs[3:5], refs[5:]
    ahead = fetch(weights, wanted(me, ring, *then), ahead_ref, sems)
    for n in range(2):
        if first:
            now[n].wait()
        part = jnp.dot(block_ref[...], now_ref[n], preferred_element_type=jnp.float32)
        outs[n][...] = part if first else seeds[n][...] + part
    for copy in ahead:
        copy.wait()


def project(me, ring, here, then, block, columns, state):
    rows, depth = block.shape
    cols = columns[0].shape[1]
    dtype = columns[0].dtype
    first = state is None
    slots = (2, depth, cols)
    sums = [jax.ShapeDtypeStruct((rows, cols), jnp.float32)] * 2
    scratch = [pltpu.VMEM(slots, dtype)] if first else []
    scratch += [pltpu.SemaphoreType.DMA((2,))] * (2 if first else 1)
    mine, theirs, ahead = pl.pallas_call(
        functools.partial(project_kernel, ring, here, then, first),
        out_shape=sums + [jax.ShapeDtypeStruct(slots, dtype)],
        in_specs=[SMEM, VMEM, HBM, HBM] + ([] if first else [VMEM] * 3),
        out_specs=[VMEM] * 3,
        scratch_shapes=scratch,
        compiler_params=PARAMS,
        cost_estimate=pl.CostEstimate(
            flops=4 * rows * depth * cols,
            bytes_accessed=2 * depth * cols * 2,
            transcendentals=0,
        ),
    )(me.reshape(1), block, *in_hbm(*columns), *(() if first else state))
    return ahead, mine, theirs


def pair_kernel(pair_ref, w_ref, mine_ref, back_ref, out_ref):
    rows = mine_ref.shape[0]
    total = mine_ref[...] + back_ref[...]
    for n in range(2):
        block = pair_ref[n * rows : (n + 1) * rows, :]
        total = total + jnp.dot(block, w_ref[n], preferred_element_type=jnp.float32)
    out_ref[...] = total.astype(out_ref.dtype)


def call(kernel, shape, dtype, args, flops):
    size = sum(a.size * a.dtype.itemsize for a in args)
    return pl.pallas_call(
        kernel,
        out_shape=jax.ShapeDtypeStruct(shape, dtype),
        in_specs=[VMEM] * len(args),
        out_specs=VMEM,
        compiler_params=PARAMS,
        cost_estimate=pl.CostEstimate(flops=flops, bytes_accessed=size, transcendentals=0),
    )(*args)


def local(queries, keys, values, gain):
    rows, width = queries.shape
    return pl.pallas_call(
        local_kernel,
        out_shape=[
            jax.ShapeDtypeStruct((width, DH), jnp.bfloat16),
            jax.ShapeDtypeStruct((rows, width), jnp.float32),
            jax.ShapeDtypeStruct((rows, width), queries.dtype),
            jax.ShapeDtypeStruct(gain.shape, gain.dtype),
        ],
        in_specs=[HBM] * 4,
        out_specs=[VMEM] * 4,
        scratch_shapes=[
            pltpu.VMEM((rows, width), keys.dtype),
            pltpu.VMEM((rows, width), values.dtype),
            pltpu.SemaphoreType.DMA((4,)),
        ],
        compiler_params=PARAMS,
        cost_estimate=pl.CostEstimate(
            flops=2 * rows * width * (DH + 2 * rows),
            bytes_accessed=3 * rows * width * 2,
            transcendentals=0,
        ),
    )(*in_hbm(queries, keys, values, gain))


def on_device(queries, keys, values, norm_gain, out_weight):
    rows, width = queries.shape
    groups = lax.axis_size("seq")
    tp = lax.axis_size("tp")
    ring = tp // 2
    me = lax.axis_index("tp")
    partner = [(j, j ^ 1) for j in range(tp)]
    onward = [
        (2 * y + c, 2 * ((y + (1, -1)[c]) % ring) + c) for y in range(ring) for c in range(2)
    ]
    across = [(s ^ 1, d) for s, d in onward]
    tie = lax.optimization_barrier

    states, within, near_queries, gain = local(
        queries, keys, values, norm_gain.reshape(1, DH)
    )
    weight, states = tie((out_weight, states))
    columns = (out_weight, lax.ppermute(weight, "tp", partner))
    slices = states.reshape(groups, width // groups, DH)
    slices = lax.all_to_all(slices, "seq", 0, 0, tiled=True)
    prefix = call(scan_kernel, slices.shape, jnp.bfloat16, (slices,), slices.size)
    prefix = lax.all_to_all(prefix, "seq", 0, 0, tiled=True).reshape(width, DH)
    own = call(
        attend_kernel,
        (rows, width),
        jnp.bfloat16,
        (near_queries, within, prefix, gain),
        2 * rows * width * DH,
    )

    halves = [[2 * y, 2 * y + 1] for y in range(ring)]
    half = (ring - 1) // 2

    def send(block, pairs):
        return lax.ppermute(block, "tp", pairs)

    def multiply(here, then, block, state):
        return project(me, ring, here, then, block, columns, state)

    first = send(own, onward)
    second = send(own, across)
    state = multiply((0, False), (1, False), own, None)
    for step in range(1, half + 1):
        first, state = tie((first, state))
        state = multiply((step, False), (step, True), first, state)
        first = send(first, onward)
        second, state = tie((second, state))
        state = multiply((step, True), (step + 1, False), second, state)
        if step < half:
            second = send(second, onward)
    ahead, mine, theirs = state
    returned = send(theirs, partner)
    first, returned = tie((first, returned))
    pair = lax.all_gather(first, "tp", axis=0, tiled=True, axis_index_groups=halves)
    return call(
        pair_kernel,
        (rows, width),
        jnp.bfloat16,
        (pair, ahead, mine, returned),
        4 * rows * width * width,
    )


def solution(mesh):
    return jax.shard_map(
        on_device,
        mesh=mesh,
        in_specs=(P("seq", "tp"), P("seq", "tp"), P("seq", "tp"), P(), P(None, "tp")),
        out_specs=P("seq", "tp"),
        check_vma=False,
    )
```

```python
import functools

import jax
import jax.numpy as jnp
from jax import lax
from jax.experimental import pallas as pl
from jax.experimental.pallas import tpu as pltpu
from jax.sharding import PartitionSpec as P

DH = 128

epsilon = 1e-06


VMEM = pl.BlockSpec(memory_space=pltpu.VMEM)
SMEM = pl.BlockSpec(memory_space=pltpu.SMEM)
PARAMS = pltpu.CompilerParams(vmem_limit_bytes=12 * 2**20)
HBM = pl.BlockSpec(memory_space=pltpu.HBM)


def local_kernel(q_hbm, k_hbm, v_hbm, g_hbm, s_ref, w_ref, q_ref, g_ref, k_ref, v_ref, sems):
    pairs = ((k_hbm, k_ref), (v_hbm, v_ref), (q_hbm, q_ref), (g_hbm, g_ref))
    copies = [pltpu.make_async_copy(a, b, sems.at[n]) for n, (a, b) in enumerate(pairs)]
    for copy in copies:
        copy.start()
    rows = q_ref.shape[0]
    heads = [slice(h, h + DH) for h in range(0, q_ref.shape[1], DH)]
    copies[0].wait()
    copies[1].wait()
    for cols in heads:
        s_ref[cols, :] = lax.dot_general(
            k_ref[:, cols],
            v_ref[:, cols],
            (((0,), (0,)), ((), ())),
            preferred_element_type=jnp.float32,
        ).astype(s_ref.dtype)
    row_ids = lax.broadcasted_iota(jnp.int32, (rows, rows), 0)
    col_ids = lax.broadcasted_iota(jnp.int32, (rows, rows), 1)
    causal = col_ids <= row_ids
    copies[2].wait()
    copies[3].wait()
    for cols in heads:
        scores = lax.dot_general(
            q_ref[:, cols],
            k_ref[:, cols],
            (((1,), (1,)), ((), ())),
            preferred_element_type=jnp.float32,
        )
        scores = jnp.where(causal, scores, 0.0).astype(jnp.bfloat16)
        w_ref[:, cols] = jnp.dot(scores, v_ref[:, cols], preferred_element_type=jnp.float32)


def scan_kernel(a_ref, p_ref):
    total = jnp.zeros(a_ref.shape[1:], jnp.float32)
    for c in range(a_ref.shape[0]):
        p_ref[c] = total.astype(p_ref.dtype)
        total = total + a_ref[c].astype(jnp.float32)


def attend_kernel(q_ref, w_ref, p_ref, g_ref, o_ref):
    for h in range(0, q_ref.shape[1], DH):
        cols = slice(h, h + DH)
        attended = jnp.dot(q_ref[:, cols], p_ref[cols, :], preferred_element_type=jnp.float32)
        attended = attended + w_ref[:, cols]
        mean = jnp.mean(attended * attended, axis=-1, keepdims=True)
        o_ref[:, cols] = (attended * lax.rsqrt(mean + epsilon) * g_ref[...]).astype(o_ref.dtype)


def source(me, ring, step, other, core=None):
    core = lax.rem(me, 2) if core is None else core
    at = lax.div(me, 2) + (jnp.where(core == 0, ring - step, step))
    return 2 * lax.rem(at, ring) + (1 - core if other else core)


def in_hbm(*arrays):
    return [pltpu.with_memory_space_constraint(a, pltpu.HBM) for a in arrays]


def fetch(weight_refs, rows, out_ref, sems):
    depth = out_ref.shape[1]
    copies = []
    for n, (w, block) in enumerate(rows):
        at = pl.multiple_of(block * depth, depth)
        source_rows = weight_refs[w].at[pl.ds(at, depth), :]
        copies.append(pltpu.make_async_copy(source_rows, out_ref.at[n], sems.at[n]))
        copies[-1].start()
    return copies


def add_products(block_ref, rows_ref, slot, seeds, outs):
    for n in range(2):
        part = jnp.dot(block_ref[...], rows_ref[slot + n], preferred_element_type=jnp.float32)
        outs[n][...] = seeds[n][...] + part if seeds else part


def first_kernel(ring, later, me_ref, block_ref, w0_ref, w1_ref, *refs):
    mine_ref, theirs_ref, ahead_ref, now_ref, now_sems, sems = refs
    me, weights = me_ref[0], (w0_ref, w1_ref)
    now = fetch(weights, [(n, me) for n in range(2)], now_ref, now_sems)
    rows = [(n, source(me, ring, *item)) for item in later for n in range(2)]
    ahead = fetch(weights, rows, ahead_ref, sems)
    for copy in now:
        copy.wait()
    add_products(block_ref, now_ref, 0, None, (mine_ref, theirs_ref))
    for copy in ahead:
        copy.wait()


def next_kernel(slot, block_ref, rows_ref, *refs):
    add_products(block_ref, rows_ref, slot, refs[:2], refs[2:])


def last_kernel(ring, slot, final, me_ref, block_ref, rows_ref, m_ref, t_ref, w_ref, *refs):
    mine_ref, theirs_ref, ahead_ref, sems = refs
    rows = [(0, source(me_ref[0], ring, *item)) for item in final]
    ahead = fetch((w_ref,), rows, ahead_ref, sems)
    add_products(block_ref, rows_ref, slot, (m_ref, t_ref), (mine_ref, theirs_ref))
    for copy in ahead:
        copy.wait()


def output_kernel(near_ref, far_ref, w_ref, mine_ref, back_ref, out_ref):
    rows = mine_ref.shape[0]
    total = mine_ref[...] + back_ref[...]
    for n in range(4):
        pair_ref = (near_ref, far_ref)[n // 2]
        block = pair_ref[n % 2 * rows : (n % 2 + 1) * rows, :]
        total = total + jnp.dot(block, w_ref[n], preferred_element_type=jnp.float32)
    out_ref[...] = total.astype(out_ref.dtype)


def project(kernel, block, columns, fetched, operands, specs, scratch):
    rows, depth = block.shape
    cols = columns[0].shape[1]
    dtype = columns[0].dtype
    outs = [jax.ShapeDtypeStruct((rows, cols), jnp.float32)] * 2
    if fetched:
        outs.append(jax.ShapeDtypeStruct((fetched, depth, cols), dtype))
        scratch = scratch + [pltpu.SemaphoreType.DMA((fetched,))]
    return pl.pallas_call(
        kernel,
        out_shape=outs,
        in_specs=specs,
        out_specs=[VMEM] * len(outs),
        scratch_shapes=scratch,
        compiler_params=PARAMS,
        cost_estimate=pl.CostEstimate(
            flops=4 * rows * depth * cols,
            bytes_accessed=(2 + fetched) * depth * cols * 2,
            transcendentals=0,
        ),
    )(*operands)


def call(kernel, shape, dtype, args, flops):
    size = sum(a.size * a.dtype.itemsize for a in args)
    return pl.pallas_call(
        kernel,
        out_shape=jax.ShapeDtypeStruct(shape, dtype),
        in_specs=[VMEM] * len(args),
        out_specs=VMEM,
        compiler_params=PARAMS,
        cost_estimate=pl.CostEstimate(flops=flops, bytes_accessed=size, transcendentals=0),
    )(*args)


def local(queries, keys, values, gain):
    rows, width = queries.shape
    return pl.pallas_call(
        local_kernel,
        out_shape=[
            jax.ShapeDtypeStruct((width, DH), jnp.bfloat16),
            jax.ShapeDtypeStruct((rows, width), jnp.float32),
            jax.ShapeDtypeStruct((rows, width), queries.dtype),
            jax.ShapeDtypeStruct(gain.shape, gain.dtype),
        ],
        in_specs=[HBM] * 4,
        out_specs=[VMEM] * 4,
        scratch_shapes=[
            pltpu.VMEM((rows, width), keys.dtype),
            pltpu.VMEM((rows, width), values.dtype),
            pltpu.SemaphoreType.DMA((4,)),
        ],
        compiler_params=PARAMS,
        cost_estimate=pl.CostEstimate(
            flops=2 * rows * width * (DH + 2 * rows),
            bytes_accessed=3 * rows * width * 2,
            transcendentals=0,
        ),
    )(*in_hbm(queries, keys, values, gain))


def on_device(queries, keys, values, norm_gain, out_weight):
    rows, width = queries.shape
    groups = lax.axis_size("seq")
    tp = lax.axis_size("tp")
    ring = tp // 2
    me = lax.axis_index("tp")
    partner = [(j, j ^ 1) for j in range(tp)]
    onward = [
        (2 * y + c, 2 * ((y + (1, -1)[c]) % ring) + c) for y in range(ring) for c in range(2)
    ]
    onward_two = [
        (2 * y + c, 2 * ((y + (2, -2)[c]) % ring) + c) for y in range(ring) for c in range(2)
    ]
    across = [(s ^ 1, d) for s, d in onward]
    tie = lax.optimization_barrier

    states, within, near_queries, gain = local(
        queries, keys, values, norm_gain.reshape(1, DH)
    )
    weight, states = tie((out_weight, states))
    columns = (out_weight, lax.ppermute(weight, "tp", partner))
    slices = states.reshape(groups, width // groups, DH)
    slices = lax.all_to_all(slices, "seq", 0, 0, tiled=True)
    prefix = call(scan_kernel, slices.shape, jnp.bfloat16, (slices,), slices.size)
    prefix = lax.all_to_all(prefix, "seq", 0, 0, tiled=True).reshape(width, DH)
    own = call(
        attend_kernel,
        (rows, width),
        jnp.bfloat16,
        (near_queries, within, prefix, gain),
        2 * rows * width * DH,
    )

    halves = [[2 * y, 2 * y + 1] for y in range(ring)]
    spot = me.reshape(1)
    order = ((1, True), (1, False), (2, False), (2, True), (3, False))
    final = ((3, True, 0), (3, True, 1), (4, False, 0), (4, False, 1))

    def send(block, pairs):
        return lax.ppermute(block, "tp", pairs)

    def share(block):
        return lax.all_gather(block, "tp", axis=0, tiled=True, axis_index_groups=halves)

    def multiply(slot, block, ahead, sums):
        return project(
            functools.partial(next_kernel, 2 * slot),
            block,
            columns,
            0,
            (block, ahead, *sums),
            [VMEM] * 4,
            [],
        )

    b1 = send(own, across)
    a2 = send(own, onward_two)
    a1 = send(own, onward)
    now = (2, width, out_weight.shape[1])
    *sums, ahead = project(
        functools.partial(first_kernel, ring, order),
        own,
        columns,
        2 * len(order),
        (spot, own, *in_hbm(*columns)),
        [SMEM, VMEM, HBM, HBM],
        [pltpu.VMEM(now, out_weight.dtype), pltpu.SemaphoreType.DMA((2,))],
    )
    b1, sums = tie((b1, sums))
    b2 = send(b1, onward)
    sums = multiply(0, b1, ahead, sums)
    sums = multiply(1, a1, ahead, sums)
    a2, sums = tie((a2, sums))
    a4 = send(a2, onward_two)
    a3 = send(a2, onward)
    sums = multiply(2, a2, ahead, sums)
    b2, sums = tie((b2, sums))
    b3 = send(b2, onward)
    sums = multiply(3, b2, ahead, sums)
    mine, theirs, rest = project(
        functools.partial(last_kernel, ring, 8, final),
        a3,
        columns,
        len(final),
        (spot, a3, ahead, *sums, *in_hbm(out_weight)),
        [SMEM, VMEM, VMEM, VMEM, VMEM, HBM],
        [],
    )
    returned = send(theirs, partner)
    near = share(b3)
    a4, near = tie((a4, near))
    far = share(a4)
    return call(
        output_kernel,
        (rows, width),
        jnp.bfloat16,
        (near, far, rest, mine, returned),
        8 * rows * width * width,
    )


def solution(mesh):
    return jax.shard_map(
        on_device,
        mesh=mesh,
        in_specs=(P("seq", "tp"), P("seq", "tp"), P("seq", "tp"), P(), P(None, "tp")),
        out_specs=P("seq", "tp"),
        check_vma=False,
    )
```

```python
import functools

import jax
import jax.numpy as jnp
from jax import lax
from jax.experimental import pallas as pl
from jax.experimental.pallas import tpu as pltpu
from jax.sharding import PartitionSpec as P

DH = 128

epsilon = 1e-06


VMEM = pl.BlockSpec(memory_space=pltpu.VMEM)
SMEM = pl.BlockSpec(memory_space=pltpu.SMEM)
PARAMS = pltpu.CompilerParams(vmem_limit_bytes=12 * 2**20)
HBM = pl.BlockSpec(memory_space=pltpu.HBM)


def local_kernel(q_hbm, k_hbm, v_hbm, g_hbm, s_ref, w_ref, q_ref, g_ref, k_ref, v_ref, sems):
    pairs = ((k_hbm, k_ref), (v_hbm, v_ref), (q_hbm, q_ref), (g_hbm, g_ref))
    copies = [pltpu.make_async_copy(a, b, sems.at[n]) for n, (a, b) in enumerate(pairs)]
    for copy in copies:
        copy.start()
    rows = q_ref.shape[0]
    heads = [slice(h, h + DH) for h in range(0, q_ref.shape[1], DH)]
    copies[0].wait()
    copies[1].wait()
    for cols in heads:
        s_ref[cols, :] = lax.dot_general(
            k_ref[:, cols],
            v_ref[:, cols],
            (((0,), (0,)), ((), ())),
            preferred_element_type=jnp.float32,
        ).astype(s_ref.dtype)
    row_ids = lax.broadcasted_iota(jnp.int32, (rows, rows), 0)
    col_ids = lax.broadcasted_iota(jnp.int32, (rows, rows), 1)
    causal = col_ids <= row_ids
    copies[2].wait()
    copies[3].wait()
    for cols in heads:
        scores = lax.dot_general(
            q_ref[:, cols],
            k_ref[:, cols],
            (((1,), (1,)), ((), ())),
            preferred_element_type=jnp.float32,
        )
        scores = jnp.where(causal, scores, 0.0).astype(jnp.bfloat16)
        w_ref[:, cols] = jnp.dot(scores, v_ref[:, cols], preferred_element_type=jnp.float32)


def scan_kernel(a_ref, p_ref):
    total = jnp.zeros(a_ref.shape[1:], jnp.float32)
    for c in range(a_ref.shape[0]):
        p_ref[c] = total.astype(p_ref.dtype)
        total = total + a_ref[c].astype(jnp.float32)


def attend_kernel(q_ref, w_ref, p_ref, g_ref, o_ref):
    for h in range(0, q_ref.shape[1], DH):
        cols = slice(h, h + DH)
        attended = jnp.dot(q_ref[:, cols], p_ref[cols, :], preferred_element_type=jnp.float32)
        attended = attended + w_ref[:, cols]
        mean = jnp.mean(attended * attended, axis=-1, keepdims=True)
        o_ref[:, cols] = (attended * lax.rsqrt(mean + epsilon) * g_ref[...]).astype(o_ref.dtype)


def source(me, ring, step, other, core=None):
    core = lax.rem(me, 2) if core is None else core
    at = lax.div(me, 2) + (jnp.where(core == 0, ring - step, step))
    return 2 * lax.rem(at, ring) + (1 - core if other else core)


def in_hbm(*arrays):
    return [pltpu.with_memory_space_constraint(a, pltpu.HBM) for a in arrays]


def fetch(weight_refs, rows, out_ref, sems):
    depth = out_ref.shape[1]
    copies = []
    for n, (w, block) in enumerate(rows):
        at = pl.multiple_of(block * depth, depth)
        source_rows = weight_refs[w].at[pl.ds(at, depth), :]
        copies.append(pltpu.make_async_copy(source_rows, out_ref.at[n], sems.at[n]))
        copies[-1].start()
    return copies


def add_products(block_ref, rows_ref, slot, seeds, outs):
    for n in range(2):
        part = jnp.dot(block_ref[...], rows_ref[slot + n], preferred_element_type=jnp.float32)
        outs[n][...] = seeds[n][...] + part if seeds else part


def first_kernel(ring, later, me_ref, block_ref, w0_ref, w1_ref, *refs):
    mine_ref, theirs_ref, ahead_ref, now_ref, now_sems, sems = refs
    me, weights = me_ref[0], (w0_ref, w1_ref)
    now = fetch(weights, [(n, me) for n in range(2)], now_ref, now_sems)
    rows = [(n, source(me, ring, *item)) for item in later for n in range(2)]
    ahead = fetch(weights, rows, ahead_ref, sems)
    for copy in now:
        copy.wait()
    add_products(block_ref, now_ref, 0, None, (mine_ref, theirs_ref))
    for copy in ahead:
        copy.wait()


def next_kernel(slot, block_ref, rows_ref, *refs):
    add_products(block_ref, rows_ref, slot, refs[:2], refs[2:])


def refill_kernel(ring, slot, later, me_ref, block_ref, rows_ref, m_ref, t_ref, *refs):
    w0_ref, w1_ref, mine_ref, theirs_ref, ahead_ref, sems = refs
    rows = [(n, source(me_ref[0], ring, *item)) for item in later for n in range(2)]
    ahead = fetch((w0_ref, w1_ref), rows, ahead_ref, sems)
    add_products(block_ref, rows_ref, slot, (m_ref, t_ref), (mine_ref, theirs_ref))
    for copy in ahead:
        copy.wait()


def closing_kernel(slot, block_ref, rows_ref, *refs):
    total = jnp.dot(block_ref[...], rows_ref[slot], preferred_element_type=jnp.float32)
    for ref in refs[:-1]:
        total = total + ref[...]
    refs[-1][...] = total.astype(refs[-1].dtype)


def project(kernel, block, columns, fetched, operands, specs, scratch):
    rows, depth = block.shape
    cols = columns[0].shape[1]
    dtype = columns[0].dtype
    outs = [jax.ShapeDtypeStruct((rows, cols), jnp.float32)] * 2
    if fetched:
        outs.append(jax.ShapeDtypeStruct((fetched, depth, cols), dtype))
        scratch = scratch + [pltpu.SemaphoreType.DMA((fetched,))]
    return pl.pallas_call(
        kernel,
        out_shape=outs,
        in_specs=specs,
        out_specs=[VMEM] * len(outs),
        scratch_shapes=scratch,
        compiler_params=PARAMS,
        cost_estimate=pl.CostEstimate(
            flops=4 * rows * depth * cols,
            bytes_accessed=(2 + fetched) * depth * cols * 2,
            transcendentals=0,
        ),
    )(*operands)


def call(kernel, shape, dtype, args, flops):
    size = sum(a.size * a.dtype.itemsize for a in args)
    return pl.pallas_call(
        kernel,
        out_shape=jax.ShapeDtypeStruct(shape, dtype),
        in_specs=[VMEM] * len(args),
        out_specs=VMEM,
        compiler_params=PARAMS,
        cost_estimate=pl.CostEstimate(flops=flops, bytes_accessed=size, transcendentals=0),
    )(*args)


def local(queries, keys, values, gain):
    rows, width = queries.shape
    return pl.pallas_call(
        local_kernel,
        out_shape=[
            jax.ShapeDtypeStruct((width, DH), jnp.bfloat16),
            jax.ShapeDtypeStruct((rows, width), jnp.float32),
            jax.ShapeDtypeStruct((rows, width), queries.dtype),
            jax.ShapeDtypeStruct(gain.shape, gain.dtype),
        ],
        in_specs=[HBM] * 4,
        out_specs=[VMEM] * 4,
        scratch_shapes=[
            pltpu.VMEM((rows, width), keys.dtype),
            pltpu.VMEM((rows, width), values.dtype),
            pltpu.SemaphoreType.DMA((4,)),
        ],
        compiler_params=PARAMS,
        cost_estimate=pl.CostEstimate(
            flops=2 * rows * width * (DH + 2 * rows),
            bytes_accessed=3 * rows * width * 2,
            transcendentals=0,
        ),
    )(*in_hbm(queries, keys, values, gain))


def on_device(queries, keys, values, norm_gain, out_weight):
    rows, width = queries.shape
    groups = lax.axis_size("seq")
    tp = lax.axis_size("tp")
    ring = tp // 2
    me = lax.axis_index("tp")
    partner = [(j, j ^ 1) for j in range(tp)]
    onward = [
        (2 * y + c, 2 * ((y + (1, -1)[c]) % ring) + c) for y in range(ring) for c in range(2)
    ]
    onward_two = [
        (2 * y + c, 2 * ((y + (2, -2)[c]) % ring) + c) for y in range(ring) for c in range(2)
    ]
    across = [(s ^ 1, d) for s, d in onward]
    tie = lax.optimization_barrier

    states, within, near_queries, gain = local(
        queries, keys, values, norm_gain.reshape(1, DH)
    )
    weight, states = tie((out_weight, states))
    columns = (out_weight, lax.ppermute(weight, "tp", partner))
    slices = states.reshape(groups, width // groups, DH)
    slices = lax.all_to_all(slices, "seq", 0, 0, tiled=True)
    prefix = call(scan_kernel, slices.shape, jnp.bfloat16, (slices,), slices.size)
    prefix = lax.all_to_all(prefix, "seq", 0, 0, tiled=True).reshape(width, DH)
    own = call(
        attend_kernel,
        (rows, width),
        jnp.bfloat16,
        (near_queries, within, prefix, gain),
        2 * rows * width * DH,
    )

    spot = me.reshape(1)
    early = ((1, True), (1, False), (2, False), (2, True))
    late = ((4, False), (3, True), (3, False))

    def send(block, pairs):
        return lax.ppermute(block, "tp", pairs)

    def multiply(slot, block, ahead, sums):
        return project(
            functools.partial(next_kernel, 2 * slot),
            block,
            columns,
            0,
            (block, ahead, *sums),
            [VMEM] * 4,
            [],
        )

    b1 = send(own, across)
    a2 = send(own, onward_two)
    a1 = send(own, onward)
    b2 = send(b1, onward)
    now = (2, width, out_weight.shape[1])
    *sums, ahead = project(
        functools.partial(first_kernel, ring, early),
        own,
        columns,
        2 * len(early),
        (spot, own, *in_hbm(*columns)),
        [SMEM, VMEM, HBM, HBM],
        [pltpu.VMEM(now, out_weight.dtype), pltpu.SemaphoreType.DMA((2,))],
    )
    a2, sums = tie((a2, sums))
    a4 = send(a2, onward_two)
    b3 = send(b2, onward)
    a3 = send(a2, onward)
    sums = multiply(0, b1, ahead, sums)
    sums = multiply(1, a1, ahead, sums)
    sums = multiply(2, a2, ahead, sums)
    *sums, ahead = project(
        functools.partial(refill_kernel, ring, 6, late),
        b2,
        columns,
        2 * len(late),
        (spot, b2, ahead, *sums, *in_hbm(*columns)),
        [SMEM, VMEM, VMEM, VMEM, VMEM, HBM, HBM],
        [],
    )
    a4, sums = tie((a4, sums))
    sums = multiply(0, a4, ahead, sums)
    b3, sums = tie((b3, sums))
    mine, theirs = multiply(1, b3, ahead, sums)
    a3, theirs = tie((a3, theirs))
    flops = 2 * rows * width * width
    shape = (rows, width)
    theirs = call(
        functools.partial(closing_kernel, 5), shape, jnp.float32, (a3, ahead, theirs), flops
    )
    returned = send(theirs, partner)
    return call(
        functools.partial(closing_kernel, 4),
        shape,
        jnp.bfloat16,
        (a3, ahead, mine, returned),
        flops,
    )


def solution(mesh):
    return jax.shard_map(
        on_device,
        mesh=mesh,
        in_specs=(P("seq", "tp"), P("seq", "tp"), P("seq", "tp"), P(), P(None, "tp")),
        out_specs=P("seq", "tp"),
        check_vma=False,
    )
```
